128 devices in a mesh: lat: 8 (over y, core), lon: 16 (over x, z).
Axes of the slice: x: 4, y: 4, z: 4, core: 2. Of those that a mesh axis runs over, the one named last changes fastest.
Arguments:
- obs_pert: bfloat16 [8192, 128, 256], P(('lat', 'lon')), may hold values from -4 to 4
- obs_dep: bfloat16 [8192, 128], P(('lat', 'lon')), may hold values from -6 to 6
- valid_rows: int32 [8192], P(('lat', 'lon')), may hold values from 1 to 128
- local_lists: int32 [512, 24], P(('lat', 'lon')), may hold values from 0 to 8191, as said below
- state_mean: float32 [8, 262144], P(None, ('lat', 'lon')), may hold values from -6 to 6
- state_pert: bfloat16 [8, 262144, 256], P(None, ('lat', 'lon')), may hold values from -6 to 6
- interp_lists: int32 [8192, 4], P(('lat', 'lon')), may hold values from 0 to 511, as said below
- interp_coef: float32 [4, 262144], P(None, ('lat', 'lon')), may hold values from 0.1 to 0.6
Outputs:
- analysis: bfloat16 [8, 262144, 256], P(None, ('lat', 'lon'))
The draws below stay inside these ranges and needn't reach their ends.
Inputs may be any that keep to these rules, and one draw needn't show every extreme that they name: `local_lists`: device i of lat+lon stores blocks i * 64 to (i + 1) * 64 - 1. Among the lists of the 4 domains of one device, at most 2 entries name blocks stored on any one device, and on every owner some device serves exactly 2. Entries may repeat. `interp_lists`: domain g is owned by device g // 4 of lat+lon. Every domain named for a tile of device (a, b) is owned by a device whose lat index differs from a by at most 1 and whose lon index differs from b by at most 1 modulo the lon axis's size.
All inputs are finite; a program needn't handle non-finite values.
Results may differ from the reference program's by a relative error of at most 0.003.
Values may be sent and summed in bfloat16 or wider, within the bound.
A program may use at most 256 MiB of HBM per device.

```python
import jax
import jax.numpy as jnp
from jax import lax

MEMBERS = 256
BLOCK_ROWS = 128
BLK_DEV = 64
DOM_DEV = 4
LIST_LEN = 24
NS_ITERS = 4
LEV = 8
TILE = 32
INTERP = 4
CAP = 2
NBLK = 8192
DOMS = 512
COLS = 262144
TILES = 8192
N_LAT = 8
N_LON = 16


def draw_local_lists(key, part):
    n_devices = DOMS // DOM_DEV
    capacity = CAP
    entries = DOM_DEV * LIST_LEN
    pool_size = n_devices * capacity

    def owner_lists(owner_key):
        key_rest = jax.random.fold_in(owner_key, 11)
        key_perm = jax.random.fold_in(owner_key, 12)
        key_local = jax.random.fold_in(owner_key, 13)
        key_order = jax.random.fold_in(owner_key, 14)
        rest = jax.random.permutation(key_rest, pool_size - capacity)[:entries - capacity] + capacity
        slots = jnp.concatenate([jnp.arange(capacity, dtype=jnp.int32), rest.astype(jnp.int32)])
        device_perm = jax.random.permutation(key_perm, n_devices).astype(jnp.int32)
        source = device_perm[slots // capacity]
        local_index = jax.random.randint(key_local, (entries,), 0, BLK_DEV, dtype=jnp.int32)
        listed = source * BLK_DEV + local_index
        order = jax.random.permutation(key_order, entries)
        return listed[order]
    owner_keys = jax.random.split(jax.random.fold_in(key, 5), n_devices)
    result = jax.vmap(owner_lists)(owner_keys)
    return result.reshape(DOMS, LIST_LEN).astype(jnp.int32)


def draw_interp_lists(key, part):
    n_devices = DOMS // DOM_DEV
    tiles_dev = TILES // n_devices
    device = jnp.arange(TILES, dtype=jnp.int32) // tiles_dev
    lat_here = device // N_LON
    lon_here = device % N_LON
    lat_step = jax.random.randint(jax.random.fold_in(key, 21), (TILES, INTERP), -1, 2, dtype=jnp.int32)
    lon_step = jax.random.randint(jax.random.fold_in(key, 22), (TILES, INTERP), -1, 2, dtype=jnp.int32)
    within = jax.random.randint(jax.random.fold_in(key, 23), (TILES, INTERP), 0, DOM_DEV, dtype=jnp.int32)
    lat_there = jnp.clip(lat_here[:, None] + lat_step, 0, N_LAT - 1)
    lon_there = (lon_here[:, None] + lon_step) % N_LON
    return ((lat_there * N_LON + lon_there) * DOM_DEV + within).astype(jnp.int32)


def place_ends(drawn, key, least, largest):
    dims = drawn.shape
    place = [jax.random.randint(jax.random.fold_in(key, axis), (), 0, dims[axis]) for axis in range(len(dims))]
    drawn = drawn.at[tuple(place)].set(least)
    longest = dims.index(max(dims))
    place[longest] = (place[longest] + 1) % dims[longest]
    return drawn.at[tuple(place)].set(largest)


def level_of(stream_key, extent, cuts, smallest, high):
    level, own = 1.0, jax.random.fold_in(stream_key, 6)
    for position, parts in cuts:
        steps = jnp.exp(jax.random.uniform(jax.random.fold_in(own, position), (parts,), jnp.float32, smallest / len(cuts), high / len(cuts)))
        level = level * jnp.repeat(steps, extent[position] // parts).reshape([-1 if axis == position else 1 for axis in range(len(extent))])
    return level


def scatter_about(key, dims, scale, limit, cuts=(), held_as=jnp.bfloat16):
    values = scale * jax.random.normal(key, dims, jnp.float32)
    if cuts:
        values = values * level_of(key, dims, cuts, -0.22, 0.18)
    return jnp.clip(values, -limit, limit).astype(held_as)


def setup_inputs(seed: int = 0) -> dict:
    key_list = jax.random.split(jax.random.key(seed), 9)
    return {
        "obs_pert": scatter_about(key_list[0], (NBLK, BLOCK_ROWS, MEMBERS), 0.5, 4.0, ((0, 128),)),
        "obs_dep": scatter_about(key_list[1], (NBLK, BLOCK_ROWS), 1.0, 6.0, ((0, 128),)),
        "valid_rows": place_ends(jax.random.randint(key_list[2], (NBLK,), 1, BLOCK_ROWS + 1), jax.random.fold_in(key_list[2], 1), 1, BLOCK_ROWS).astype(jnp.int32),
        "local_lists": draw_local_lists(jax.random.fold_in(key_list[8], 71), 0),
        "state_mean": scatter_about(key_list[4], (LEV, COLS), 1.0, 6.0, ((1, 128),), jnp.float32),
        "state_pert": scatter_about(key_list[5], (LEV, COLS, MEMBERS), 1.0, 6.0, ((1, 128),)),
        "interp_lists": draw_interp_lists(jax.random.fold_in(key_list[8], 71), 0),
        "interp_coef": jnp.clip(0.1 + 0.5 * jax.random.uniform(key_list[7], (INTERP, COLS), jnp.float32) ** level_of(key_list[7], (INTERP, COLS), ((1, 128),), -0.2, 0.2), 0.1, 0.6),
    }


def make_weights(gram, innov, members):
    identity = jnp.eye(members, dtype=jnp.float32)
    system = (members - 1.0) * identity + gram
    scale = jnp.sqrt(lax.optimization_barrier(jnp.sum(system * system, axis=(-2, -1))))[..., None, None]
    approx = system / scale
    inverse_root = jnp.broadcast_to(identity, system.shape)
    for sweep in range(NS_ITERS):
        factor = 1.5 * identity - 0.5 * jnp.matmul(inverse_root, approx, precision=lax.Precision.HIGHEST)
        approx = jnp.matmul(approx, factor, precision=lax.Precision.HIGHEST)
        inverse_root = jnp.matmul(factor, inverse_root, precision=lax.Precision.HIGHEST)
    inner = jnp.matmul(inverse_root, innov[..., None], precision=lax.Precision.HIGHEST)
    mean_weight = jnp.matmul(inverse_root, inner, precision=lax.Precision.HIGHEST) / scale
    return (jnp.sqrt((members - 1.0) / scale) * inverse_root + mean_weight).astype(jnp.bfloat16)

def reference(obs_pert, obs_dep, valid_rows, local_lists, state_mean, state_pert, interp_lists, interp_coef):
    block_rows = obs_pert.shape[1]
    members = obs_pert.shape[2]
    keep = jnp.arange(block_rows)[None, :] < valid_rows[:, None]
    masked_pert = jnp.where(keep[:, :, None], obs_pert, jnp.zeros((), jnp.bfloat16))
    masked_dep = jnp.where(keep, obs_dep, jnp.zeros((), jnp.bfloat16))

    def one_domain(listed):
        blocks = masked_pert[listed].astype(jnp.float32)
        departs = masked_dep[listed].astype(jnp.float32)
        gram = jnp.einsum('lri,lrj->ij', blocks, blocks, precision=lax.Precision.HIGHEST)
        innov = jnp.einsum('lri,lr->i', blocks, departs, precision=lax.Precision.HIGHEST)
        return make_weights(gram, innov, members)
    weights = lax.map(one_domain, local_lists)
    levels = state_pert.shape[0]
    columns = state_pert.shape[1]
    groups = DOMS // DOM_DEV
    per_group = columns // groups
    tiles_group = per_group // TILE
    grouped_pert = jnp.transpose(state_pert.reshape(levels, groups, tiles_group, TILE, members), (1, 0, 2, 3, 4))
    grouped_mean = jnp.transpose(state_mean.reshape(levels, groups, tiles_group, TILE), (1, 0, 2, 3))
    grouped_coef = jnp.transpose(interp_coef.reshape(INTERP, groups, tiles_group, TILE), (1, 0, 2, 3))
    grouped_lists = interp_lists.reshape(groups, tiles_group, INTERP)

    def one_group(pieces):
        perturbed, mean_here, coef_here, lists_here = pieces
        pert_float = perturbed.astype(jnp.float32)
        total = mean_here[..., None]
        for corner in range(INTERP):
            chosen = weights[lists_here[:, corner]].astype(jnp.float32)
            product = jnp.einsum('ltci,tij->ltcj', pert_float, chosen, precision=lax.Precision.HIGHEST)
            total = total + coef_here[corner][None, :, :, None] * product
        return total.astype(jnp.bfloat16)
    result = lax.map(one_group, (grouped_pert, grouped_mean, grouped_coef, grouped_lists))
    return jnp.transpose(result, (1, 0, 2, 3, 4)).reshape(levels, columns, members)
```

```python
import jax
import jax.numpy as jnp
from jax import lax
from jax.experimental import pallas as pl
from jax.experimental.pallas import tpu as pltpu
from jax.sharding import PartitionSpec as P

NS_ITERS = 4
TILE = 32


def neighbours(block, axis, periodic):
    count = lax.axis_size(axis)
    forward = [(i, i + 1) for i in range(count - 1)]
    if periodic:
        forward.append((count - 1, 0))
    backward = [(target, source) for source, target in forward]
    return lax.ppermute(block, axis, forward), block, lax.ppermute(block, axis, backward)


def split(a):
    high = a.astype(jnp.bfloat16)
    low = (a - high.astype(jnp.float32)).astype(jnp.bfloat16)
    return high, low


def product(a, b):
    (a_high, a_low), (b_high, b_low) = a, b
    small = jnp.dot(a_high, b_low, preferred_element_type=jnp.float32)
    small += jnp.dot(a_low, b_high, preferred_element_type=jnp.float32)
    return small + jnp.dot(a_high, b_high, preferred_element_type=jnp.float32)


def weights_kernel(slots, blocks, departs, out, held, sems):
    domains, rows, members = held.shape
    entries = sems.shape[0]
    list_len = entries // domains
    block_rows = rows // list_len

    def fetch(e):
        d, l = e // list_len, e % list_len
        return pltpu.make_async_copy(
            blocks.at[slots[e]],
            held.at[d, pl.ds(pl.multiple_of(l * block_rows, block_rows), block_rows), :],
            sems.at[e],
        )

    @pl.loop(0, entries)
    def _(e):
        fetch(e).start()

    @pl.loop(0, domains)
    def _(d):
        @pl.loop(0, list_len)
        def _(l):
            fetch(d * list_len + l).wait()

        listed = held[d]
        gram = lax.dot_general(
            listed, listed, (((0,), (0,)), ((), ())), preferred_element_type=jnp.float32
        )
        innov = jnp.dot(departs[d], listed, preferred_element_type=jnp.float32)
        innov = jnp.transpose(jnp.broadcast_to(innov[:1], (128, members)))
        row = lax.broadcasted_iota(jnp.int32, (members, members), 0)
        column = lax.broadcasted_iota(jnp.int32, (members, members), 1)
        identity = (row == column).astype(jnp.float32)
        system = (members - 1.0) * identity + gram
        scale = jnp.sqrt(jnp.sum(system * system, keepdims=True))
        approx = system / scale
        root = None
        for sweep in range(NS_ITERS):
            approx_parts = split(approx)
            if root is None:
                factor = 1.5 * identity - 0.5 * approx
                factor_parts = split(factor)
                root = factor
            else:
                root_parts = split(root)
                factor = 1.5 * identity - 0.5 * product(root_parts, approx_parts)
                factor_parts = split(factor)
                root = product(factor_parts, root_parts)
            if sweep < NS_ITERS - 1:
                approx = product(approx_parts, factor_parts)
        root_parts = split(root)
        inner = product(root_parts, split(innov))
        mean_weight = product(root_parts, split(inner)) / scale
        gain = jnp.sqrt((members - 1.0) / scale)
        for part in range(members // 128):
            lanes = slice(part * 128, part * 128 + 128)
            out[d, :, lanes] = (gain * root[:, lanes] + mean_weight).astype(jnp.bfloat16)


def make_weights(slots, blocks, departs, domains):
    entries = slots.shape[0]
    block_rows, members = blocks.shape[1:]
    rows = entries // domains * block_rows
    wide = jnp.broadcast_to(departs.reshape(domains, 1, rows), (domains, 16, rows))
    return pl.pallas_call(
        weights_kernel,
        out_shape=jax.ShapeDtypeStruct((domains, members, members), jnp.bfloat16),
        grid_spec=pltpu.PrefetchScalarGridSpec(
            num_scalar_prefetch=1,
            grid=(),
            in_specs=[
                pl.BlockSpec(memory_space=pl.ANY),
                pl.BlockSpec(memory_space=pltpu.VMEM),
            ],
            out_specs=pl.BlockSpec(memory_space=pltpu.VMEM),
            scratch_shapes=[
                pltpu.VMEM((domains, rows, members), jnp.bfloat16),
                pltpu.SemaphoreType.DMA((entries,)),
            ],
        ),
        compiler_params=pltpu.CompilerParams(vmem_limit_bytes=40 << 20),
        name="weights",
    )(slots, blocks, wide)


def interp_kernel(position, low, middle, high, perturbed, terms, out, tiles, sems):
    step = pl.program_id(0)
    levels, columns, members = perturbed.shape
    near = middle.shape[0]
    per_step = columns // TILE
    n_interp = terms.shape[1] - levels

    @pl.when(step == 0)
    def _():
        copies = [
            pltpu.make_async_copy(ref, tiles.at[pl.ds(i * near, near)], sems.at[i])
            for i, ref in enumerate((low, middle, high))
        ]
        for copy in copies:
            copy.start()
        for copy in copies:
            copy.wait()

    for t in range(per_step):
        cols = slice(t * TILE, t * TILE + TILE)
        x = perturbed[:, cols, :].reshape(levels * TILE, members)
        total = None
        for corner in range(n_interp):
            chosen = tiles[position[(step * per_step + t) * n_interp + corner]]
            moved = jnp.dot(x, chosen, preferred_element_type=jnp.float32)
            moved = moved.reshape(levels, TILE, members)
            coef = jnp.broadcast_to(
                terms[cols, levels + corner : levels + corner + 1], (TILE, members)
            )
            total = coef[None] * moved if total is None else total + coef[None] * moved
        for level in range(levels):
            mean = jnp.broadcast_to(terms[cols, level : level + 1], (TILE, members))
            out[level, cols, :] = (mean + total[level]).astype(jnp.bfloat16)


def interpolate(position, near, state_pert, terms, per_step):
    levels, cols_here, members = state_pert.shape
    columns = per_step * TILE
    return pl.pallas_call(
        interp_kernel,
        out_shape=jax.ShapeDtypeStruct(state_pert.shape, jnp.bfloat16),
        grid_spec=pltpu.PrefetchScalarGridSpec(
            num_scalar_prefetch=1,
            grid=(cols_here // columns,),
            in_specs=[pl.BlockSpec(memory_space=pl.ANY)] * 3
            + [
                pl.BlockSpec((levels, columns, members), lambda i, p: (0, i, 0)),
                pl.BlockSpec((columns, terms.shape[1]), lambda i, p: (i, 0)),
            ],
            out_specs=pl.BlockSpec((levels, columns, members), lambda i, p: (0, i, 0)),
            scratch_shapes=[
                pltpu.VMEM((3 * near[1].shape[0], members, members), jnp.bfloat16),
                pltpu.SemaphoreType.DMA((3,)),
            ],
        ),
        compiler_params=pltpu.CompilerParams(vmem_limit_bytes=40 << 20),
        name="interp",
    )(position, *near, state_pert, terms)


def local(
    obs_pert, obs_dep, valid_rows, local_lists, state_mean, state_pert, interp_lists, interp_coef
):
    n_devices = lax.axis_size(("lat", "lon"))
    n_lon = lax.axis_size("lon")
    blocks_here, block_rows, members = obs_pert.shape
    keep = jnp.arange(block_rows)[None, :] < valid_rows[:, None]
    masked_pert = jnp.where(keep[:, :, None], obs_pert, jnp.zeros((), jnp.bfloat16))
    masked_dep = jnp.where(keep, obs_dep, jnp.zeros((), jnp.bfloat16))
    capacity = 2 * max(1, 64 // n_devices)
    domains_here, list_len = local_lists.shape
    entries = local_lists.reshape(-1)
    source = entries // blocks_here
    local_index = entries % blocks_here
    onehot = (source[:, None] == jnp.arange(n_devices, dtype=jnp.int32)[None, :]).astype(jnp.int32)
    earlier = jnp.cumsum(onehot, axis=0) - onehot
    slot = jnp.sum(earlier * onehot, axis=1)
    flat_slot = source * capacity + slot
    request = jnp.zeros((n_devices * capacity,), jnp.int32).at[flat_slot].set(local_index)
    asked = lax.all_to_all(
        request.reshape(n_devices, capacity),
        ("lat", "lon"),
        split_axis=0,
        concat_axis=0,
        tiled=True,
    ).reshape(-1)
    out_pert = masked_pert[asked].reshape(n_devices, capacity, block_rows, members)
    out_dep = masked_dep[asked].reshape(n_devices, capacity, block_rows)
    arrived = (
        lax.all_to_all(out_pert, ("lat", "lon"), split_axis=0, concat_axis=0, tiled=True),
        lax.all_to_all(out_dep, ("lat", "lon"), split_axis=0, concat_axis=0, tiled=True),
    )
    got_dep = arrived[1].reshape(-1, block_rows)[flat_slot]
    weights = make_weights(
        flat_slot, arrived[0].reshape(-1, block_rows, members), got_dep, domains_here
    )
    beside = jnp.concatenate(neighbours(weights, "lon", True), axis=0)
    near = neighbours(beside, "lat", False)
    owner = interp_lists // domains_here
    within = interp_lists % domains_here
    lat_step = owner // n_lon - lax.axis_index("lat")
    lon_step = (owner % n_lon - lax.axis_index("lon") + 1) % n_lon - 1
    position = ((lat_step + 1) * 3 + lon_step + 1) * domains_here + within
    terms = jnp.concatenate([state_mean, interp_coef], axis=0).T
    return interpolate(position.reshape(-1), near, state_pert, terms, 4)


def solution(mesh):
    in_specs = (
        P(("lat", "lon"), None, None),
        P(("lat", "lon"), None),
        P(("lat", "lon")),
        P(("lat", "lon"), None),
        P(None, ("lat", "lon")),
        P(None, ("lat", "lon"), None),
        P(("lat", "lon"), None),
        P(None, ("lat", "lon")),
    )
    out_specs = P(None, ("lat", "lon"), None)
    return jax.shard_map(local, mesh=mesh, in_specs=in_specs, out_specs=out_specs, check_vma=False)
```
